32 devices in a mesh: row: 8 (over y, x, core), col: 4 (over z).
Axes of the slice: x: 2, y: 2, z: 4, core: 2. Of those that a mesh axis runs over, the one named last changes fastest.
Arguments:
- matrix: float32 [16384, 16384], P('row', 'col'), may hold values from -8 to 8, as said below
- vectors: float32 [16384, 8192], P('row', 'col'), may hold values from -6 to 6
Outputs:
- updated: float32 [16384, 16384], P('row', 'col')
- rotated: float32 [16384, 8192], P('row', 'col')
The draws below stay inside these ranges and needn't reach their ends.
Inputs may be any that keep to these rules, and one draw needn't show every extreme that they name: matrix is symmetric up to rounding.
All inputs are finite; a program needn't handle non-finite values.
Results may differ from the reference program's by a relative error of at most 0.00011.
Values sent between devices are 32-bit elements; how exact they have to be, the bound alone decides.
A program may use at most 192 MiB of HBM per device.

```python
import jax
import jax.numpy as jnp
from jax import lax

M = 16384
B = 256
NE = 8192


def draw_matrix(key, part):
    first_key = jax.random.fold_in(key, 11)
    normal_draw = jax.random.normal(first_key, (M, M), jnp.float32)
    symmetric = (normal_draw + normal_draw.T) * 0.7071067811865476
    return jnp.clip(symmetric, -8.0, 8.0)


def level_of(own_key, dims, cuts, low, high):
    loudness, own = 1.0, jax.random.fold_in(own_key, 6)
    for dim, shards_of in cuts:
        heights = jnp.exp(jax.random.uniform(jax.random.fold_in(own, dim), (shards_of,), jnp.float32, low / len(cuts), high / len(cuts)))
        loudness = loudness * jnp.repeat(heights, dims[dim] // shards_of).reshape([-1 if axis == dim else 1 for axis in range(len(dims))])
    return loudness


def centred(own_key, shape, deviation, limit, shards=(), held_as=jnp.bfloat16):
    array = jax.random.normal(own_key, shape, jnp.float32) * deviation
    if len(shards) > 0:
        array = level_of(own_key, shape, shards, -0.22, 0.18) * array
    return jnp.clip(array, min=-limit, max=limit).astype(held_as)


def setup_inputs(seed: int = 0) -> dict:
    keys = jax.random.split(jax.random.key(seed), 3)
    return {
        "matrix": draw_matrix(jax.random.fold_in(keys[2], 71), 0),
        "vectors": centred(keys[1], (M, NE), 1.0, 6.0, ((0, 8), (1, 4)), jnp.float32),
    }


def matmul(left, right):
    return jnp.dot(left.astype(jnp.float32), right.astype(jnp.float32), preferred_element_type=jnp.float32, precision=lax.Precision.HIGHEST)

def reference(matrix, vectors):
    row_ids = jnp.arange(M, dtype=jnp.int32)
    panel = jnp.where(row_ids[:, None] >= B, matrix[:, :B], jnp.float32(0.0))
    gram = matmul(panel.T, panel)
    factor = jnp.linalg.cholesky(gram)
    basis = lax.linalg.triangular_solve(factor, panel, left_side=False, lower=True, transpose_a=True)
    product = matmul(matrix, basis)
    coupling = matmul(basis.T, product)
    wide = 2.0 * product - 2.0 * matmul(basis, coupling)
    updated = matrix - matmul(basis, wide.T) - matmul(wide, basis.T)
    mixing = matmul(basis.T, vectors)
    rotated = vectors - 2.0 * matmul(basis, mixing)
    return (updated, rotated)
```

```python
import jax
import jax.numpy as jnp
from jax import lax
from jax.sharding import PartitionSpec as P

B = 256
CHUNKS = 8
HIGH = lax.Precision.HIGH
HIGHEST = lax.Precision.HIGHEST


def dot(left, right, contract=(1, 0), precision=HIGH):
    return lax.dot_general(
        left,
        right,
        (((contract[0],), (contract[1],)), ((), ())),
        preferred_element_type=jnp.float32,
        precision=precision,
    )


def bit_of(axis, bit):
    return (lax.axis_index(axis) >> bit) & 1


def flip(axis, size, bit):
    return lambda x: lax.ppermute(x, axis, [(i, i ^ (1 << bit)) for i in range(size)])


def join(own, other, mine):
    upper = mine == 1
    return jnp.concatenate([jnp.where(upper, other, own), jnp.where(upper, own, other)], axis=0)


def half_of(x, which):
    half = x.shape[0] // 2
    return lax.dynamic_slice_in_dim(x, which * half, half, axis=0)


def reduce_over(x, axis, size, bits):
    for bit in bits:
        mine = bit_of(axis, bit)
        received = flip(axis, size, bit)(half_of(x, 1 - mine))
        x = half_of(x, mine) + received
    for bit in reversed(bits):
        x = join(x, flip(axis, size, bit)(x), bit_of(axis, bit))
    return x


def sum_rows(x, axis, size):
    n_bits = size.bit_length() - 1
    mine = bit_of(axis, 0)
    received = flip(axis, size, 0)(half_of(x, 1 - mine))
    x = half_of(x, mine) + received
    rest = list(range(1, n_bits))
    half = x.shape[0] // 2
    low = reduce_over(x[:half], axis, size, rest)
    high = reduce_over(x[half:], axis, size, rest[::-1])
    x = jnp.concatenate([low, high], axis=0)
    return join(x, flip(axis, size, 0)(x), mine)


def spread_bits(x, axis, size, bits):
    reached = [0]
    for bit in bits:
        half = x.shape[0] // 2
        received = lax.ppermute(x[half:], axis, [(i, i | (1 << bit)) for i in reached])
        x = jnp.where(bit_of(axis, bit) == 1, received, x[:half])
        reached = reached + [i | (1 << bit) for i in reached]
    for bit in reversed(bits):
        received = lax.ppermute(x, axis, [(i, i ^ (1 << bit)) for i in reached])
        x = join(x, received, bit_of(axis, bit))
    received = lax.ppermute(x, axis, [(i, i | 1) for i in reached])
    return jnp.where(bit_of(axis, 0) == 1, received, x)


def spread(x, axis, size):
    rest = list(range(1, size.bit_length() - 1))
    half = x.shape[0] // 2
    return jnp.concatenate(
        [
            spread_bits(x[:half], axis, size, rest),
            spread_bits(x[half:], axis, size, rest[::-1]),
        ],
        axis=0,
    )


def chain(x, axis, size):
    if size == 1:
        return x
    place = lax.axis_index(axis)
    rows = x.shape[0] // CHUNKS
    steps = CHUNKS + size - 2
    onward = [(i, i + 1) for i in range(size - 1)]
    received, arrivals = None, []
    for step in range(steps):
        own = x[min(step, CHUNKS - 1) * rows : (min(step, CHUNKS - 1) + 1) * rows]
        sent = own if received is None else jnp.where(place == 0, own, received)
        received = lax.ppermute(sent, axis, onward)
        arrivals.append(received)
    arrived = lax.dynamic_slice_in_dim(
        jnp.concatenate(arrivals, axis=0), jnp.maximum(place - 1, 0) * rows, rows * CHUNKS, axis=0
    )
    return jnp.where(place == 0, x, arrived)


def make_body(n_row, n_col):
    def body(matrix, vectors):
        rows_here, columns_here = matrix.shape
        row_ids = lax.axis_index("row") * rows_here + jnp.arange(rows_here, dtype=jnp.int32)
        column_ids = lax.axis_index("col") * columns_here + jnp.arange(columns_here, dtype=jnp.int32)
        own_rows = jnp.where(row_ids[:, None] >= B, matrix[:, :B], jnp.float32(0.0))
        own_columns = jnp.where(column_ids[None, :] >= B, matrix[:B, :], jnp.float32(0.0))
        panel_columns = spread(own_columns, "row", n_row)
        panel_rows = chain(own_rows, "col", n_col)

        gram = lax.psum(dot(panel_columns, panel_columns, (1, 1), HIGHEST), "col")
        partial_rows = dot(matrix, panel_columns, (1, 1))
        factor = jnp.linalg.cholesky(gram)
        inverse = lax.linalg.triangular_solve(
            factor, jnp.eye(B, dtype=jnp.float32), left_side=True, lower=True
        )
        raw_rows = reduce_over(partial_rows, "col", n_col, list(range(n_col.bit_length() - 1)))
        raw_coupling = lax.psum(dot(panel_rows, partial_rows, (0, 0)), ("row", "col"))
        raw_mixing = sum_rows(dot(panel_rows, vectors, (0, 0)), "row", n_row)
        raw_columns = sum_rows(dot(panel_rows, matrix, (0, 0)), "row", n_row)

        coupling = dot(dot(inverse, raw_coupling, (1, 0), HIGHEST), inverse, (1, 1), HIGHEST)
        basis_rows = dot(panel_rows, inverse, (1, 1))
        basis_columns = dot(inverse, panel_columns)
        wide_rows = 2.0 * (dot(raw_rows, inverse, (1, 1)) - dot(basis_rows, coupling))
        wide_columns = 2.0 * (dot(inverse, raw_columns) - dot(coupling, basis_columns, (0, 0)))
        mixing = 2.0 * dot(inverse, raw_mixing)
        rotated = vectors - dot(basis_rows, mixing)
        updated = matrix - dot(
            jnp.concatenate([basis_rows, wide_rows], axis=1),
            jnp.concatenate([wide_columns, basis_columns], axis=0),
        )
        return (updated, rotated)

    return body


def solution(mesh):
    placed = (P("row", "col"), P("row", "col"))
    return jax.shard_map(
        make_body(mesh.shape["row"], mesh.shape["col"]),
        mesh=mesh,
        in_specs=placed,
        out_specs=(P("row", "col"), P("row", "col")),
        check_vma=False,
    )
```

```python
import jax
import jax.numpy as jnp
from jax import lax
from jax.sharding import PartitionSpec as P

B = 256
HIGH = lax.Precision.HIGH
HIGHEST = lax.Precision.HIGHEST


def dot(left, right, contract=(1, 0), precision=HIGH):
    return lax.dot_general(
        left,
        right,
        (((contract[0],), (contract[1],)), ((), ())),
        preferred_element_type=jnp.float32,
        precision=precision,
    )


def bit_of(axis, bit):
    return (lax.axis_index(axis) >> bit) & 1


def flip(axis, size, bit):
    return lambda x: lax.ppermute(x, axis, [(i, i ^ (1 << bit)) for i in range(size)])


def join(own, other, mine):
    upper = mine == 1
    return jnp.concatenate([jnp.where(upper, other, own), jnp.where(upper, own, other)], axis=0)


def half_of(x, which):
    half = x.shape[0] // 2
    return lax.dynamic_slice_in_dim(x, which * half, half, axis=0)


def beside(send, flips, state, work):
    send, state = lax.optimization_barrier((send, state))
    received = [each(x) for each, x in zip(flips, send)]
    if work:
        state = work.pop(0)(state)
        received, state = lax.optimization_barrier((received, state))
    return received, state


def sum_rows(x, axis, size, state, work):
    work = list(work)
    mine = bit_of(axis, 0)
    received = flip(axis, size, 0)(half_of(x, 1 - mine))
    x = half_of(x, mine) + received
    rest = list(range(1, size.bit_length() - 1))
    half = x.shape[0] // 2
    parts = [x[:half], x[half:]]
    steps = list(zip(rest, rest[::-1]))
    for bits in steps:
        sides = [bit_of(axis, bit) for bit in bits]
        flips = [flip(axis, size, bit) for bit in bits]
        received, state = beside([half_of(p, 1 - m) for p, m in zip(parts, sides)], flips, state, work)
        parts = [half_of(p, m) + r for p, m, r in zip(parts, sides, received)]
    for bits in reversed(steps):
        flips = [flip(axis, size, bit) for bit in bits]
        received, state = beside(parts, flips, state, work)
        parts = [join(p, r, bit_of(axis, bit)) for p, r, bit in zip(parts, received, bits)]
    x = jnp.concatenate(parts, axis=0)
    x = join(x, flip(axis, size, 0)(x), mine)
    for piece in work:
        state = piece(state)
    return x, state


def lower_inverse(factor):
    return lax.linalg.triangular_solve(
        factor, jnp.eye(factor.shape[0], dtype=jnp.float32), left_side=True, lower=True
    )


def factor_first(state):
    (gram,) = state
    half = gram.shape[0] // 2
    return gram, jnp.linalg.cholesky(gram[:half, :half])


def invert_first(state):
    gram, first = state
    half = gram.shape[0] // 2
    inverse = lower_inverse(first)
    below = dot(gram[half:, :half], inverse, (1, 1), HIGHEST)
    return inverse, below, gram[half:, half:] - dot(below, below, (1, 1), HIGHEST)


def factor_second(state):
    inverse, below, rest = state
    return inverse, below, jnp.linalg.cholesky(rest)


def invert_second(state):
    first, below, factor = state
    second = lower_inverse(factor)
    corner = -dot(dot(second, below, (1, 0), HIGHEST), first, (1, 0), HIGHEST)
    top = jnp.concatenate([first, jnp.zeros_like(first)], axis=1)
    return (jnp.concatenate([top, jnp.concatenate([corner, second], axis=1)], axis=0),)


def spread_bits(x, axis, size, bits):
    reached = [0]
    for bit in bits:
        half = x.shape[0] // 2
        received = lax.ppermute(x[half:], axis, [(i, i | (1 << bit)) for i in reached])
        x = jnp.where(bit_of(axis, bit) == 1, received, x[:half])
        reached = reached + [i | (1 << bit) for i in reached]
    for bit in reversed(bits):
        received = lax.ppermute(x, axis, [(i, i ^ (1 << bit)) for i in reached])
        x = join(x, received, bit_of(axis, bit))
    received = lax.ppermute(x, axis, [(i, i | 1) for i in reached])
    return jnp.where(bit_of(axis, 0) == 1, received, x)


def spread(x, axis, size):
    rest = list(range(1, size.bit_length() - 1))
    half = x.shape[0] // 2
    return jnp.concatenate(
        [
            spread_bits(x[:half], axis, size, rest),
            spread_bits(x[half:], axis, size, rest[::-1]),
        ],
        axis=0,
    )


def add_over(x, axis, size):
    for bit in range(size.bit_length() - 1):
        x = x + flip(axis, size, bit)(x)
    return x


def make_body(n_row, n_col):
    def body(matrix, vectors):
        rows_here, columns_here = matrix.shape
        row_ids = lax.axis_index("row") * rows_here + jnp.arange(rows_here, dtype=jnp.int32)
        column_ids = lax.axis_index("col") * columns_here + jnp.arange(columns_here, dtype=jnp.int32)
        own_rows = jnp.where(row_ids[:, None] >= B, matrix[:, :B], jnp.float32(0.0))
        own_columns = jnp.where(column_ids[None, :] >= B, matrix[:B, :], jnp.float32(0.0))
        at_root = lax.axis_index("col") == 0
        root_rows = jnp.where(at_root, own_rows, jnp.float32(0.0))
        root_rows, own_columns = lax.optimization_barrier((root_rows, own_columns))
        panel_rows = lax.psum(root_rows, "col")
        panel_columns = spread(own_columns, "row", n_row)

        partial_rows = dot(matrix, panel_columns, (1, 1))
        partial_gram = dot(panel_columns, panel_columns, (1, 1), HIGHEST)
        panel_rows, partial_rows = lax.optimization_barrier((panel_rows, partial_rows))
        raw_rows = lax.psum(partial_rows, "col")
        gram = add_over(partial_gram, "col", n_col)
        partial_sums = jnp.concatenate(
            [
                dot(panel_rows, matrix, (0, 0)),
                dot(panel_rows, vectors, (0, 0)),
                dot(panel_rows, partial_rows, (0, 0)),
            ],
            axis=1,
        )
        sums, (inverse,) = sum_rows(
            partial_sums,
            "row",
            n_row,
            (gram,),
            [factor_first, invert_first, factor_second, invert_second],
        )
        raw_columns = sums[:, :columns_here]
        raw_mixing = sums[:, columns_here:-B]
        raw_coupling = add_over(sums[:, -B:], "col", n_col)

        coupling = dot(dot(inverse, raw_coupling, (1, 0), HIGHEST), inverse, (1, 1), HIGHEST)
        basis_rows = dot(panel_rows, inverse, (1, 1))
        basis_columns = dot(inverse, panel_columns)
        wide_rows = 2.0 * (dot(raw_rows, inverse, (1, 1)) - dot(basis_rows, coupling))
        wide_columns = 2.0 * (dot(inverse, raw_columns) - dot(coupling, basis_columns, (0, 0)))
        mixing = 2.0 * dot(inverse, raw_mixing)
        rotated = vectors - dot(basis_rows, mixing)
        updated = matrix - dot(
            jnp.concatenate([basis_rows, wide_rows], axis=1),
            jnp.concatenate([wide_columns, basis_columns], axis=0),
        )
        return (updated, rotated)

    return body


def solution(mesh):
    placed = (P("row", "col"), P("row", "col"))
    return jax.shard_map(
        make_body(mesh.shape["row"], mesh.shape["col"]),
        mesh=mesh,
        in_specs=placed,
        out_specs=(P("row", "col"), P("row", "col")),
        check_vma=False,
    )
```
